32 devices in a mesh: trade: 2 (over y), date: 4 (over z), path: 4 (over x, core).
Axes of the slice: x: 2, y: 2, z: 4, core: 2. Of those that a mesh axis runs over, the one named last changes fastest.
Arguments:
- trade_values: bfloat16 [1280, 64, 512], P('trade', 'date', 'path'), parts along dimension 2, may hold values from -4 to 4
- set_of_trade: int32 [1280], P('trade'), may hold values from 0 to 255, as said below
- thresholds: float32 [256], replicated, may hold values from 0.2 to 2
- spreads: float32 [256], replicated, may hold values from 0.003 to 0.03
- retention: float32 [256, 64], replicated, may hold values from 0 to 1, as said below
Outputs:
- net_exposure: float32 [256, 64, 512], P('trade', 'date', 'path'), parts along dimension 2
- funding: float32 [256, 64, 512], P('trade', 'date', 'path'), parts along dimension 2
The draws below stay inside these ranges and needn't reach their ends.
There are 4 independent parts, one for each index of `path`. The reference program is written for one: setup_inputs(seed, part) draws one part's arguments, and reference() takes and returns one part's arrays. A program takes and returns all parts, laid end to end along the dimension named above; an argument that names none is the same for every part. Nothing has to cross between parts.
Inputs may be any that keep to these rules, and one draw needn't show every extreme that they name: `set_of_trade`: trade n lies in trade block b = n // 640; it names a set of set block b (sets b * 128 to (b + 1) * 128 - 1) or of set block (b + 1) mod (2). The first 128 trades of block b name the sets of set block b in order. `retention`: strictly between 0 and 1.
All inputs are finite; a program needn't handle non-finite values.
Results may differ from the reference program's by a relative error of at most 0.0003.
Values sent between devices are 32-bit elements; how exact they have to be, the bound alone decides.
No kernel may reach another device: no remote copies, remote signals or barrier semaphores. Data moves between devices by JAX's collectives and lax.ppermute only.
A program may use at most 64 MiB of HBM per device.

```python
import math
import jax
import jax.numpy as jnp
from jax import lax

TR_DEV = 640
SET_DEV = 128
PATHS = 128
LAG = 10
TRADES = 1280
SETS = 256
EVOLUTION_DATES = 64


def draw_set_of_trade(key, part):
    random_keys = jax.random.split(jax.random.fold_in(key, 11), 2)
    blocks = SETS // SET_DEV
    number = jnp.arange(TRADES, dtype=jnp.int32)
    block = number // TR_DEV
    place = number % TR_DEV
    inner = jax.random.randint(random_keys[0], (TRADES,), 0, SET_DEV, dtype=jnp.int32)
    hop = jax.random.randint(random_keys[1], (TRADES,), 0, 5, dtype=jnp.int32) == 0
    target = jnp.where(hop, (block + 1) % blocks, block)
    leading = place < SET_DEV
    target = jnp.where(leading, block, target)
    inner = jnp.where(leading, place, inner)
    return (target * SET_DEV + inner).astype(jnp.int32)


def draw_retention(key, part):
    random_keys = jax.random.split(jax.random.fold_in(key, 7), 6)
    fast_share = 0.5
    fast = jax.random.bernoulli(random_keys[0], fast_share, (SETS,))
    horizon = jax.random.uniform(random_keys[1], (SETS,), jnp.float32, 30.0, 50.0)
    keeping = jax.random.uniform(random_keys[2], (SETS,), jnp.float32, 0.4, 0.9)
    rate = jnp.where(fast, 1.0 / horizon, -jnp.log(keeping) / EVOLUTION_DATES)
    jitter = jax.random.uniform(random_keys[3], (SETS, EVOLUTION_DATES), jnp.float32, 0.5, 1.5)
    decay_factor = jnp.exp(-rate[:, None] * jitter)
    jump_event_dates = jax.random.randint(random_keys[4], (2,), 0, EVOLUTION_DATES)
    recursion_depth = jax.random.uniform(random_keys[5], (SETS, 2), jnp.float32, 0.55, 0.8)
    market_marks = jnp.arange(EVOLUTION_DATES)[:, None] == jump_event_dates[None, :]
    jump_events = jnp.prod(jnp.where(market_marks[None, :, :], recursion_depth[:, None, :], 1.0), axis=2)
    return (decay_factor * jump_events).astype(jnp.float32)


def level_of(key, dims, cuts, low, top_value):
    level, own = 1.0, jax.random.fold_in(key, 6)
    for dim, shards_of in cuts:
        draws = jnp.exp(jax.random.uniform(jax.random.fold_in(own, dim), (shards_of,), jnp.float32, low / len(cuts), top_value / len(cuts)))
        level = level * jnp.repeat(draws, dims[dim] // shards_of).reshape([-1 if axis == dim else 1 for axis in range(len(dims))])
    return level


def gaussian(rng, extent, spread, bound, cuts=(), held_as=jnp.bfloat16):
    values = spread * jax.random.normal(rng, extent, jnp.float32)
    if cuts:
        values = values * level_of(rng, extent, cuts, -0.22, 0.18)
    return jnp.clip(values, -bound, bound).astype(held_as)


def setup_inputs(seed: int = 0, part: int = 0) -> dict:
    streams_of = jax.random.split(jax.random.key(seed), 6)
    part_splits = jax.random.split(jax.random.fold_in(streams_of[5], part), 6)
    trade_values = gaussian(part_splits[0], (TRADES, EVOLUTION_DATES, PATHS), 0.5, 4.0, ((0, 2), (1, 4)))
    set_of_trade = draw_set_of_trade(jax.random.fold_in(streams_of[5], 71), part)
    thresholds = jnp.clip(jnp.exp(jax.random.uniform(streams_of[2], (SETS,), jnp.float32, math.log(0.2), math.log(2.0))), 0.2, 2.0)
    spreads = jnp.clip(jnp.exp(jax.random.uniform(streams_of[3], (SETS,), jnp.float32, math.log(0.003), math.log(0.03))), 0.003, 0.03)
    retention = draw_retention(jax.random.fold_in(streams_of[5], 71), part)
    return dict(trade_values=trade_values, set_of_trade=set_of_trade, thresholds=thresholds, spreads=spreads, retention=retention)


def reference(trade_values, set_of_trade, thresholds, spreads, retention):
    sums = jax.ops.segment_sum(trade_values.astype(jnp.float32), set_of_trade, num_segments=SETS)
    zeros = jnp.zeros((SETS, LAG, PATHS), jnp.float32)
    lagged = jnp.concatenate([zeros, sums[:, :EVOLUTION_DATES - LAG]], axis=1)
    level = thresholds[:, None, None]
    collateral = jnp.maximum(lagged - level, 0.0) - jnp.maximum(-lagged - level, 0.0)
    net_exposure = sums - collateral
    costs = spreads[:, None, None] * jnp.maximum(net_exposure, 0.0)

    def advance(state, inputs):
        rate, cost = inputs
        state = rate[:, None] * state + cost
        return state, state

    start = jnp.zeros((SETS, PATHS), jnp.float32)
    _, funding = lax.scan(advance, start, (retention.T, jnp.moveaxis(costs, 1, 0)))
    return net_exposure, jnp.moveaxis(funding, 0, 1)
```

```python
import functools

import jax
import jax.numpy as jnp
from jax import lax
from jax.experimental import pallas as pl
from jax.experimental.pallas import tpu as pltpu
from jax.sharding import PartitionSpec as P

LAG = 10
GRANT = 12 * 1024 * 1024
RIM_PIECES = (3, 4, 3)


def shifted(value, axis, steps):
    count = lax.axis_size(axis)
    return lax.ppermute(value, axis, [(i, i + steps) for i in range(count - steps)])


def from_behind(value, axis):
    count = lax.axis_size(axis)
    return lax.ppermute(value, axis, [(i, (i + 1) % count) for i in range(count)])


def exchanged(value, axis, bit):
    count = lax.axis_size(axis)
    return lax.ppermute(value, axis, [(i, i ^ bit) for i in range(count) if i ^ bit < count])


def row_sums(labels, rows, values):
    place = lax.broadcasted_iota(jnp.int32, (rows, labels.shape[0]), 0)
    selector = (place == labels[None, :]).astype(jnp.bfloat16)
    return jnp.einsum("sn,ntp->tsp", selector, values, preferred_element_type=jnp.float32)


def whole(count):
    return [pl.BlockSpec(memory_space=pltpu.VMEM)] * count


def spread_kernel(at_ref, rates_ref, level_ref, spread_ref, rate_out, slab_out, level_out, spread_out):
    dates_dev, sets, paths = rate_out.shape
    slabs = slab_out.shape[0]
    across = (sets, paths)
    column = jnp.transpose(rates_ref[pl.ds(pl.multiple_of(at_ref[0], 8), dates_dev), :])
    for t in range(dates_dev):
        rate_out[t] = jnp.broadcast_to(column[:, t : t + 1], across)
    level_out[...] = jnp.broadcast_to(jnp.transpose(level_ref[...])[:, :1], across)
    spread_out[...] = jnp.broadcast_to(jnp.transpose(spread_ref[...])[:, :1], across)
    for d in range(slabs):
        total = rates_ref[d * dates_dev : d * dates_dev + 1, :]
        for t in range(1, dates_dev):
            total = total * rates_ref[d * dates_dev + t : d * dates_dev + t + 1, :]
        full = jnp.transpose(jnp.broadcast_to(total, (8, sets)))
        slab_out[d] = jnp.broadcast_to(full[:, :1], across)


def lay_across(date_start, rates, level, spread, dates_dev, paths):
    dates, sets = rates.shape
    slabs = dates // dates_dev
    f32 = jnp.float32
    shapes = [(dates_dev, sets, paths), (slabs, sets, paths), (sets, paths), (sets, paths)]
    return pl.pallas_call(
        spread_kernel,
        out_shape=[jax.ShapeDtypeStruct(s, f32) for s in shapes],
        in_specs=[pl.BlockSpec(memory_space=pltpu.SMEM)] + whole(3),
        out_specs=whole(4),
        compiler_params=pltpu.CompilerParams(vmem_limit_bytes=GRANT),
        name="lay_across",
    )(date_start, rates, jnp.broadcast_to(level, (8, sets)), jnp.broadcast_to(spread, (8, sets)))


def gather_dates(refs):
    return [(ref, i) for ref in refs for i in range(ref.shape[0])]


def cost_kernel(split, *refs):
    early, late, rims, level_ref, spread_ref, rate_ref, cost_out, last_out = unpack(split, refs)
    sums = early + late
    sets, paths = level_ref.shape
    block = 32

    def body(j, _):
        rows = pl.ds(pl.multiple_of(j * block, block), block)
        level, spread = level_ref[rows, :], spread_ref[rows, :]
        held = []
        state = jnp.zeros((block, paths), jnp.float32)
        for t in range(len(sums)):
            now = sums[t](rows)
            held.append(now)
            lagged = rims[t](rows) if t < LAG else held[t - LAG]
            exposure = net(now, lagged, level)
            cost = spread * jnp.maximum(exposure, 0.0)
            cost_out[t, rows, :] = cost
            state = rate_ref[t, rows, :] * state + cost
        last_out[rows, :] = state
        return 0

    lax.fori_loop(0, sets // block, body, 0)


def exposure_kernel(split, *refs):
    early, late, rims, level_ref, out = unpack(split, refs)
    sums = early + late
    sets, paths = level_ref.shape
    dates_dev = len(sums)
    block = 32

    def body(j, _):
        start = pl.multiple_of(j * block, block)
        rows = pl.ds(start, block)
        level = level_ref[rows, :]
        held = []
        for t in range(dates_dev):
            now = sums[t](rows)
            held.append(now)
            lagged = rims[t](rows) if t < LAG else held[t - LAG]
            out[pl.ds(start * dates_dev + t, block, stride=dates_dev), :] = net(now, lagged, level)
        return 0

    lax.fori_loop(0, sets // block, body, 0)


def net(now, lagged, level):
    return now - (jnp.maximum(lagged - level, 0.0) - jnp.maximum(-lagged - level, 0.0))


def unpack(split, refs):
    rim_count, early_dates = split
    own_ref, other_ref = refs[:2]
    late_refs = refs[2 : 2 + rim_count]
    rim_refs = refs[2 + rim_count : 2 + 2 * rim_count]

    def added(t):
        return lambda rows: own_ref[t, rows, :] + other_ref[t, rows, :]

    def plain(ref, i):
        return lambda rows: ref[i, rows, :]

    early = [added(t) for t in range(early_dates)]
    late = [plain(ref, i) for ref, i in gather_dates(late_refs)]
    rims = [plain(ref, i) for ref, i in gather_dates(rim_refs)]
    return (early, late, rims, *refs[2 + 2 * rim_count :])


def funding_kernel(carry_ref, cost_ref, rate_ref, out):
    dates_dev, sets, paths = cost_ref.shape
    block = 32

    def body(j, _):
        start = pl.multiple_of(j * block, block)
        rows = pl.ds(start, block)
        state = carry_ref[rows, :]
        for t in range(dates_dev):
            state = rate_ref[t, rows, :] * state + cost_ref[t, rows, :]
            out[pl.ds(start * dates_dev + t, block, stride=dates_dev), :] = state
        return 0

    lax.fori_loop(0, sets // block, body, 0)


def carry_in(last, slab_rates, axis):
    count, mine = lax.axis_size(axis), lax.axis_index(axis)
    entering = jnp.zeros_like(last)
    group, before = last, jnp.ones_like(last)
    group_rate = lax.dynamic_index_in_dim(slab_rates, mine, 0, keepdims=False)
    bit = 1
    while bit < count:
        other = exchanged(group, axis, bit)
        upper = (mine & bit) != 0
        if 2 * bit < count:
            base = (mine // (2 * bit)) * (2 * bit) + bit
            upper_rate = functools.reduce(
                jnp.multiply,
                [lax.dynamic_index_in_dim(slab_rates, base + i, 0, keepdims=False) for i in range(bit)],
            )
        entering = jnp.where(upper, entering + before * other, entering)
        if 2 * bit < count:
            base = (mine // (2 * bit)) * (2 * bit)
            lower_rate = functools.reduce(
                jnp.multiply,
                [lax.dynamic_index_in_dim(slab_rates, base + i, 0, keepdims=False) for i in range(bit)],
            )
            group = jnp.where(upper, group + upper_rate * other, other + upper_rate * group)
            before = jnp.where(upper, before * lower_rate, before)
        bit *= 2
    return entering


def shards(trade_values, set_of_trade, thresholds, spreads, retention):
    set_count = thresholds.shape[0]
    dates_dev, paths = trade_values.shape[1:]
    trade_pos, date_pos = lax.axis_index("trade"), lax.axis_index("date")
    sets = set_count // lax.axis_size("trade")
    first_set = trade_pos * sets
    offset = set_of_trade - first_set
    offset = jnp.where(offset < 0, offset + set_count, offset)
    early_dates = dates_dev - LAG

    f32 = jnp.float32
    bounds = [early_dates]
    for size in RIM_PIECES:
        bounds.append(bounds[-1] + size)
    spans = list(zip(bounds[:-1], bounds[1:]))

    def arriving(span):
        part = row_sums(offset - sets, sets, trade_values[:, span[0] : span[1]])
        return from_behind(part, "trade")

    own = row_sums(offset, sets, trade_values)
    late, rims = [], []
    for span in spans:
        sums = own[span[0] : span[1]] + arriving(span)
        late.append(sums)
        rims.append(shifted(sums, "date", 1))
    other = arriving((0, early_dates))

    level = lax.dynamic_slice_in_dim(thresholds, first_set, sets)
    spread = lax.dynamic_slice_in_dim(spreads, first_set, sets)
    rates = lax.dynamic_slice_in_dim(retention.T, first_set, sets, 1)
    date_start = (date_pos * dates_dev)[None].astype(jnp.int32)
    rate_all, slab_rates, level_all, spread_all = lay_across(
        date_start, rates, level, spread, dates_dev, paths
    )

    split = (len(spans), early_dates)
    flat = jax.ShapeDtypeStruct((sets * dates_dev, paths), f32)
    tall = jax.ShapeDtypeStruct((dates_dev, sets, paths), f32)
    parts = (own, other, *late, *rims)
    costs, last = pl.pallas_call(
        functools.partial(cost_kernel, split),
        out_shape=[tall, jax.ShapeDtypeStruct((sets, paths), f32)],
        in_specs=whole(len(parts) + 3),
        out_specs=whole(2),
        compiler_params=pltpu.CompilerParams(vmem_limit_bytes=GRANT),
        name="costs",
    )(*parts, level_all, spread_all, rate_all)
    net_exposure = pl.pallas_call(
        functools.partial(exposure_kernel, split),
        out_shape=flat,
        in_specs=whole(len(parts) + 1),
        out_specs=pl.BlockSpec(memory_space=pltpu.VMEM),
        compiler_params=pltpu.CompilerParams(vmem_limit_bytes=GRANT),
        name="exposure",
    )(*parts, level_all)
    carry = carry_in(last, slab_rates, "date")
    funding = pl.pallas_call(
        funding_kernel,
        out_shape=flat,
        in_specs=whole(3),
        out_specs=pl.BlockSpec(memory_space=pltpu.VMEM),
        compiler_params=pltpu.CompilerParams(vmem_limit_bytes=GRANT),
        name="funding",
    )(carry, costs, rate_all)
    shape = (sets, dates_dev, paths)
    return net_exposure.reshape(shape), funding.reshape(shape)


def solution(mesh):
    return jax.shard_map(
        shards,
        mesh=mesh,
        in_specs=(P("trade", "date", "path"), P("trade"), P(), P(), P()),
        out_specs=(P("trade", "date", "path"), P("trade", "date", "path")),
        check_vma=False,
    )
```

```python
import functools

import jax
import jax.numpy as jnp
from jax import lax
from jax.experimental import pallas as pl
from jax.experimental.pallas import tpu as pltpu
from jax.sharding import PartitionSpec as P


LAG = 10
GRANT = 8 * 1024 * 1024
RIM_PIECES = (3, 3, 4)
BLOCK = 32


def ahead(value, axis):
    count = lax.axis_size(axis)
    return lax.ppermute(value, axis, [(i, (i + 1) % count) for i in range(count)])


def exchanged(value, axis, bit):
    return lax.ppermute(value, axis, [(i, i ^ bit) for i in range(lax.axis_size(axis))])


def row_sums(labels, rows, values):
    place = lax.broadcasted_iota(jnp.int32, (rows, labels.shape[0]), 0)
    selector = (place == labels[None, :]).astype(jnp.bfloat16)
    return jnp.einsum("sn,ntp->tsp", selector, values, preferred_element_type=jnp.float32)


def call(body, operands, shapes, scratch=(), to_hbm=False):
    vmem = pl.BlockSpec(memory_space=pltpu.VMEM)
    out = pl.BlockSpec(memory_space=pl.ANY) if to_hbm else vmem
    moved = sum(a.size for a in operands) + sum(s[0] * s[1] for s in shapes)
    return pl.pallas_call(
        body,
        out_shape=[jax.ShapeDtypeStruct(s, jnp.float32) for s in shapes],
        in_specs=[vmem] * len(operands),
        out_specs=[out] * len(shapes),
        scratch_shapes=list(scratch),
        compiler_params=pltpu.CompilerParams(vmem_limit_bytes=GRANT),
        cost_estimate=pl.CostEstimate(flops=8 * moved, bytes_accessed=4 * moved, transcendentals=0),
    )(*operands)


def prepare_kernel(rates_ref, level_ref, spread_ref, rate_out, level_out, spread_out, coef_out, slab_ref):
    dates_dev, sets, paths = rate_out.shape
    count, mine = lax.axis_size("date"), lax.axis_index("date")
    trade = lax.axis_index("trade")
    lanes = pl.ds(pl.multiple_of(trade * sets, sets), sets)

    def across(row):
        return jnp.broadcast_to(jnp.transpose(jnp.broadcast_to(row, (8, sets)))[:, :1], (sets, paths))

    here = rates_ref[pl.ds(pl.multiple_of(mine * dates_dev, dates_dev), dates_dev), lanes]
    columns = jnp.transpose(here)
    for t in range(dates_dev):
        rate_out[t] = jnp.broadcast_to(columns[:, t : t + 1], (sets, paths))
    level_out[...] = across(level_ref[pl.ds(trade, 1), :])
    spread_out[...] = across(spread_ref[pl.ds(trade, 1), :])
    for d in range(count):
        total = rates_ref[pl.ds(d * dates_dev, 1), lanes]
        for t in range(1, dates_dev):
            total = total * rates_ref[pl.ds(d * dates_dev + t, 1), lanes]
        slab_ref[pl.ds(d, 1), :] = total

    def product(base, length):
        total = slab_ref[pl.ds(base, 1), :]
        for i in range(1, length):
            total = total * slab_ref[pl.ds(base + i, 1), :]
        return total

    before, bit, stage = jnp.ones((1, sets), jnp.float32), 1, 0
    while bit < count:
        base = mine - mine % (2 * bit)
        coef_out[2 * stage] = across(before)
        coef_out[2 * stage + 1] = across(product(base + bit, bit))
        before = jnp.where(mine % (2 * bit) >= bit, before * product(base, bit), before)
        bit, stage = 2 * bit, stage + 1


def net(now, lagged, level):
    return now - (jnp.maximum(lagged - level, 0.0) - jnp.maximum(-lagged - level, 0.0))


def dates_of(refs):
    return [(ref, i) for ref in refs for i in range(ref.shape[0])]


def readers(split, refs, first):
    rim_count, early_dates = split
    own_ref, other_ref = refs[:2]
    late_refs = refs[2 : 2 + rim_count]
    rim_refs = refs[2 + rim_count : 2 + 2 * rim_count]

    def added(t):
        return lambda rows: own_ref[t, rows, :] + other_ref[t, rows, :]

    def plain(ref, i):
        return lambda rows: ref[i, rows, :]

    def masked(ref, i):
        return lambda rows: jnp.where(first, 0.0, ref[i, rows, :])

    sums = [added(t) for t in range(early_dates)] + [plain(*at) for at in dates_of(late_refs)]
    rims = [masked(*at) for at in dates_of(rim_refs)]
    return sums, rims, refs[2 + 2 * rim_count :]


def cost_kernel(split, *refs):
    first = lax.axis_index("date") == 0
    sums, rims, (level_ref, spread_ref, rate_ref, cost_out, last_out) = readers(split, refs, first)
    sets, paths = level_ref.shape
    for start in range(0, sets, BLOCK):
        rows = pl.ds(start, BLOCK)
        level, spread = level_ref[rows, :], spread_ref[rows, :]
        held = []
        state = jnp.zeros((BLOCK, paths), jnp.float32)
        for t in range(len(sums)):
            held.append(sums[t](rows))
            lagged = rims[t](rows) if t < LAG else held[t - LAG]
            cost = spread * jnp.maximum(net(held[t], lagged, level), 0.0)
            cost_out[t, rows, :] = cost
            state = rate_ref[t, rows, :] * state + cost
        last_out[rows, :] = state


def sent_out(out, held_ref, sem, start, dates_dev):
    rows = pl.ds(start * dates_dev, BLOCK * dates_dev)
    return pltpu.make_async_copy(held_ref.at[rows, :], out.at[rows, :], sem.at[start // BLOCK])


def exposure_kernel(split, *refs):
    first = lax.axis_index("date") == 0
    sums, rims, (level_ref, out, held_ref, sem) = readers(split, refs, first)
    sets, _ = level_ref.shape
    dates_dev = len(sums)
    for start in range(0, sets, BLOCK):
        rows = pl.ds(start, BLOCK)
        level = level_ref[rows, :]
        held = []
        for t in range(dates_dev):
            held.append(sums[t](rows))
            lagged = rims[t](rows) if t < LAG else held[t - LAG]
            held_ref[pl.ds(start * dates_dev + t, BLOCK, stride=dates_dev), :] = net(held[t], lagged, level)
        sent_out(out, held_ref, sem, start, dates_dev).start()
    for start in range(0, sets, BLOCK):
        sent_out(out, held_ref, sem, start, dates_dev).wait()


def join_kernel(bit, group_ref, other_ref, rate_ref, out):
    upper = lax.axis_index("date") % (2 * bit) >= bit
    group, other, rate = group_ref[...], other_ref[...], rate_ref[...]
    earlier, later = jnp.where(upper, other, group), jnp.where(upper, group, other)
    out[...] = rate * earlier + later


def funding_kernel(stages, *refs):
    others = refs[:stages]
    coef_ref, cost_ref, rate_ref, out, held_ref, sem = refs[stages:]
    dates_dev, sets, paths = cost_ref.shape
    mine = lax.axis_index("date")
    for start in range(0, sets, BLOCK):
        rows = pl.ds(start, BLOCK)
        state = jnp.zeros((BLOCK, paths), jnp.float32)
        for stage in range(stages):
            upper = mine % (2 << stage) >= (1 << stage)
            longer = state + coef_ref[2 * stage, rows, :] * others[stage][rows, :]
            state = jnp.where(upper, longer, state)
        for t in range(dates_dev):
            state = rate_ref[t, rows, :] * state + cost_ref[t, rows, :]
            held_ref[pl.ds(start * dates_dev + t, BLOCK, stride=dates_dev), :] = state
        sent_out(out, held_ref, sem, start, dates_dev).start()
    for start in range(0, sets, BLOCK):
        sent_out(out, held_ref, sem, start, dates_dev).wait()


def shards(trade_values, set_of_trade, thresholds, spreads, retention):
    set_count = thresholds.shape[0]
    dates_dev, paths = trade_values.shape[1:]
    n_trade = lax.axis_size("trade")
    sets = set_count // n_trade
    offset = set_of_trade - lax.axis_index("trade") * sets
    offset = jnp.where(offset < 0, offset + set_count, offset)
    early_dates = dates_dev - LAG
    bounds = [early_dates]
    for size in RIM_PIECES:
        bounds.append(bounds[-1] + size)
    spans = list(zip(bounds[:-1], bounds[1:]))

    cross = lax.optimization_barrier(row_sums(offset - sets, sets, trade_values))
    late_in = []
    for low, high in spans:
        late_in.append(ahead(cross[low:high], "trade"))
    other = ahead(cross[:early_dates], "trade")
    own = row_sums(offset, sets, trade_values)
    late, rims = [], []
    for k, (low, high) in enumerate(spans):
        mine = own if k == 0 else lax.optimization_barrier((own, late[-1]))[0]
        sums = mine[low:high] + late_in[k]
        rims.append(ahead(sums, "date"))
        late.append(sums)

    count = lax.axis_size("date")
    stages = count.bit_length() - 1
    tall, wide, flat = (dates_dev, sets, paths), (sets, paths), (sets * dates_dev, paths)
    rate_all, level_all, spread_all, coefs = call(
        prepare_kernel,
        (retention.T, thresholds.reshape(n_trade, sets), spreads.reshape(n_trade, sets)),
        (tall, wide, wide, (2 * stages, *wide)),
        [pltpu.VMEM((count, sets), jnp.float32)],
    )

    split = (len(spans), early_dates)
    parts = (own, other, *late, *rims)
    blocks = sets // BLOCK
    leaving = [pltpu.VMEM(flat, jnp.float32), pltpu.SemaphoreType.DMA((blocks,))]
    costs, group = call(functools.partial(cost_kernel, split), (*parts, level_all, spread_all, rate_all), (tall, wide))
    (net_exposure,) = call(functools.partial(exposure_kernel, split), (*parts, level_all), (flat,), leaving, True)
    others = []
    for stage in range(stages):
        others.append(exchanged(group, "date", 1 << stage))
        if stage + 1 < stages:
            (group,) = call(
                functools.partial(join_kernel, 1 << stage), (group, others[-1], coefs[2 * stage + 1]), (wide,)
            )
    (funding,) = call(
        functools.partial(funding_kernel, stages), (*others, coefs, costs, rate_all), (flat,), leaving, True
    )
    shape = (sets, dates_dev, paths)
    return net_exposure.reshape(shape), funding.reshape(shape)


def solution(mesh):
    return jax.shard_map(
        shards,
        mesh=mesh,
        in_specs=(P("trade", "date", "path"), P("trade"), P(), P(), P()),
        out_specs=(P("trade", "date", "path"), P("trade", "date", "path")),
        check_vma=False,
    )
```

```python
import functools

import jax
import jax.numpy as jnp
from jax import lax
from jax.experimental import pallas as pl
from jax.experimental.pallas import tpu as pltpu
from jax.sharding import PartitionSpec as P


LAG = 10
GRANT = 8 * 1024 * 1024
LAST_PART = 2
BLOCK = 32


def ahead(value, axis):
    count = lax.axis_size(axis)
    return lax.ppermute(value, axis, [(i, (i + 1) % count) for i in range(count)])


def exchanged(value, axis, bit):
    return lax.ppermute(value, axis, [(i, i ^ bit) for i in range(lax.axis_size(axis))])


def row_sums(labels, rows, values):
    place = lax.broadcasted_iota(jnp.int32, (rows, labels.shape[0]), 0)
    selector = (place == labels[None, :]).astype(jnp.bfloat16)
    return jnp.einsum("sn,ntp->tsp", selector, values, preferred_element_type=jnp.float32)


def group_bounds(sets):
    cut = sets - sets // LAST_PART
    return [(0, cut), (cut, sets)]


def call(body, operands, shapes, scratch=(), to_hbm=False, into=None):
    vmem, hbm = pl.BlockSpec(memory_space=pltpu.VMEM), pl.BlockSpec(memory_space=pl.ANY)
    out = hbm if to_hbm else vmem
    kept = () if into is None else (into,)
    moved = sum(a.size for a in operands) + sum(s[0] * s[1] for s in shapes)
    return pl.pallas_call(
        body,
        out_shape=[jax.ShapeDtypeStruct(s, jnp.float32) for s in shapes],
        in_specs=[vmem] * len(operands) + [hbm] * len(kept),
        out_specs=[out] * len(shapes),
        scratch_shapes=list(scratch),
        compiler_params=pltpu.CompilerParams(vmem_limit_bytes=GRANT),
        cost_estimate=pl.CostEstimate(flops=8 * moved, bytes_accessed=4 * moved, transcendentals=0),
        input_output_aliases={len(operands): 0} if kept else {},
    )(*operands, *kept)


def prepare_kernel(rates_ref, level_ref, spread_ref, rate_out, level_out, spread_out, coef_out, slab_ref):
    dates_dev, sets, paths = rate_out.shape
    count, mine = lax.axis_size("date"), lax.axis_index("date")
    trade = lax.axis_index("trade")
    lanes = pl.ds(pl.multiple_of(trade * sets, sets), sets)

    def across(row):
        return jnp.broadcast_to(jnp.transpose(jnp.broadcast_to(row, (8, sets)))[:, :1], (sets, paths))

    here = rates_ref[pl.ds(pl.multiple_of(mine * dates_dev, dates_dev), dates_dev), lanes]
    columns = jnp.transpose(here)
    for t in range(dates_dev):
        rate_out[t] = jnp.broadcast_to(columns[:, t : t + 1], (sets, paths))
    level_out[...] = across(level_ref[pl.ds(trade, 1), :])
    spread_out[...] = across(spread_ref[pl.ds(trade, 1), :])
    for d in range(count):
        total = rates_ref[pl.ds(d * dates_dev, 1), lanes]
        for t in range(1, dates_dev):
            total = total * rates_ref[pl.ds(d * dates_dev + t, 1), lanes]
        slab_ref[pl.ds(d, 1), :] = total

    bit, stage = count // 2, 0
    while bit:
        base = mine - mine % (2 * bit)
        lower = beyond = jnp.ones((1, sets), jnp.float32)
        for i in range(bit):
            rate = slab_ref[pl.ds(base + i, 1), :]
            lower = lower * rate
            beyond = beyond * jnp.where(base + i > mine, rate, 1.0)
        coef_out[2 * stage] = across(lower)
        coef_out[2 * stage + 1] = across(beyond)
        bit, stage = bit // 2, stage + 1


def net(now, lagged, level):
    return now - (jnp.maximum(lagged - level, 0.0) - jnp.maximum(-lagged - level, 0.0))


def exposures(begin, pieces, refs, use):
    own_ref, other_ref = refs[:2]
    late_refs, rim_refs = refs[2 : 2 + pieces], refs[2 + pieces : 2 + 2 * pieces]
    level_ref = refs[2 + 2 * pieces]
    first = lax.axis_index("date") == 0
    early = other_ref.shape[0]
    dates_dev = own_ref.shape[0]
    for piece in range(pieces):
        inside = pl.ds(piece * BLOCK, BLOCK)
        rows = pl.ds(begin + piece * BLOCK, BLOCK)
        level = level_ref[rows, :]
        held, found = [], []
        for t in range(dates_dev):
            if t < early:
                held.append(own_ref[t, rows, :] + other_ref[t, inside, :])
            else:
                held.append(late_refs[piece][t - early])
            lagged = held[t - LAG] if t >= LAG else jnp.where(first, 0.0, rim_refs[piece][t])
            found.append(net(held[t], lagged, level))
        use(piece, inside, rows, found)


def cost_kernel(begin, pieces, *refs):
    spread_ref, rate_ref, coef_ref, cost_out, last_out, sent_out_ref = refs[3 + 2 * pieces :]

    def use(piece, inside, rows, found):
        spread = spread_ref[rows, :]
        state = jnp.zeros_like(spread)
        for t, exposure in enumerate(found):
            cost = spread * jnp.maximum(exposure, 0.0)
            cost_out[t, inside, :] = cost
            state = rate_ref[t, rows, :] * state + cost
        last_out[inside, :] = state
        sent_out_ref[inside, :] = state * coef_ref[1, rows, :]

    exposures(begin, pieces, refs, use)


def sent_out(out, held_ref, sem, begin, piece, dates_dev):
    rows = pl.ds(piece * BLOCK * dates_dev, BLOCK * dates_dev)
    there = pl.ds((begin + piece * BLOCK) * dates_dev, BLOCK * dates_dev)
    return pltpu.make_async_copy(held_ref.at[rows, :], out.at[there, :], sem.at[piece])


def exposure_kernel(begin, pieces, *refs):
    out, held_ref, sem = refs[-3:]
    dates_dev = refs[0].shape[0]

    def use(piece, inside, rows, found):
        for t, exposure in enumerate(found):
            held_ref[pl.ds(piece * BLOCK * dates_dev + t, BLOCK, stride=dates_dev), :] = exposure
        sent_out(out, held_ref, sem, begin, piece, dates_dev).start()

    exposures(begin, pieces, refs, use)
    for piece in range(pieces):
        sent_out(out, held_ref, sem, begin, piece, dates_dev).wait()


def entering(stages, others, coef_ref, inside, rows):
    mine, count = lax.axis_index("date"), lax.axis_size("date")
    arrived = jnp.where(mine >= count // 2, others[0][inside, :], 0.0)
    for stage in range(1, stages):
        upper = mine & (count >> (stage + 1)) != 0
        kept = jnp.where(upper, arrived * coef_ref[2 * stage, rows, :], arrived)
        arrived = kept + others[stage][inside, :]
    return arrived


def join_kernel(begin, stage, last_ref, coef_ref, *refs):
    inside, rows = pl.ds(0, last_ref.shape[0]), pl.ds(begin, last_ref.shape[0])
    arrived = entering(stage, refs[:-1], coef_ref, inside, rows)
    longer = arrived * coef_ref[2 * stage, rows, :] + last_ref[...] * coef_ref[2 * stage + 1, rows, :]
    upper = lax.axis_index("date") & (lax.axis_size("date") >> (stage + 1)) != 0
    refs[-1][...] = jnp.where(upper, arrived, longer)


def funding_kernel(begin, pieces, stages, *refs):
    coef_ref, cost_ref, rate_ref = refs[stages : stages + 3]
    out, held_ref, sem = refs[-3:]
    dates_dev = rate_ref.shape[0]
    for piece in range(pieces):
        inside = pl.ds(piece * BLOCK, BLOCK)
        rows = pl.ds(begin + piece * BLOCK, BLOCK)
        state = entering(stages, refs[:stages], coef_ref, inside, rows)
        for t in range(dates_dev):
            state = rate_ref[t, rows, :] * state + cost_ref[t, inside, :]
            held_ref[pl.ds(piece * BLOCK * dates_dev + t, BLOCK, stride=dates_dev), :] = state
        sent_out(out, held_ref, sem, begin, piece, dates_dev).start()
    for piece in range(pieces):
        sent_out(out, held_ref, sem, begin, piece, dates_dev).wait()


def shards(trade_values, set_of_trade, thresholds, spreads, retention):
    set_count = thresholds.shape[0]
    dates_dev, paths = trade_values.shape[1:]
    n_trade = lax.axis_size("trade")
    sets = set_count // n_trade
    offset = set_of_trade - lax.axis_index("trade") * sets
    offset = jnp.where(offset < 0, offset + set_count, offset)
    early = dates_dev - LAG
    pieces = [slice(low, low + BLOCK) for low in range(0, sets, BLOCK)]
    groups = group_bounds(sets)

    cross = lax.optimization_barrier(row_sums(offset - sets, sets, trade_values))
    late_in, other = [], []
    for rows in pieces:
        late_in.append(ahead(cross[early:, rows], "trade"))
    for low, high in groups:
        other.append(ahead(cross[:early, low:high], "trade"))
    own = row_sums(offset, sets, trade_values)
    late, rims = [], []
    for k, rows in enumerate(pieces):
        mine = own if k == 0 else lax.optimization_barrier((own, late[-1]))[0]
        sums = mine[early:, rows] + late_in[k]
        rims.append(ahead(sums, "date"))
        late.append(sums)

    count = lax.axis_size("date")
    stages = count.bit_length() - 1
    tall, wide = (dates_dev, sets, paths), (sets, paths)
    rate_all, level_all, spread_all, coefs = call(
        prepare_kernel,
        (retention.T, thresholds.reshape(n_trade, sets), spreads.reshape(n_trade, sets)),
        (tall, wide, wide, (2 * stages, *wide)),
        [pltpu.VMEM((count, sets), jnp.float32)],
    )

    flat = (sets * dates_dev, paths)
    net_exposure = funding = None
    for g, (low, high) in enumerate(groups):
        size = high - low
        mine = range(low // BLOCK, high // BLOCK)
        parts = (own, other[g], *[late[k] for k in mine], *[rims[k] for k in mine], level_all)
        leaving = [pltpu.VMEM((size * dates_dev, paths), jnp.float32), pltpu.SemaphoreType.DMA((len(mine),))]
        costs, last, sent = call(
            functools.partial(cost_kernel, low, len(mine)),
            (*parts, spread_all, rate_all, coefs),
            ((dates_dev, size, paths), (size, paths), (size, paths)),
        )
        net_exposure = call(
            functools.partial(exposure_kernel, low, len(mine)), parts, (flat,), leaving, True, net_exposure
        )[0]
        others = []
        for stage in range(stages):
            if stage:
                (sent,) = call(functools.partial(join_kernel, low, stage), (last, coefs, *others), ((size, paths),))
            others.append(exchanged(sent, "date", count >> (stage + 1)))
        funding = call(
            functools.partial(funding_kernel, low, len(mine), stages),
            (*others, coefs, costs, rate_all),
            (flat,),
            leaving,
            True,
            funding,
        )[0]
    shape = (sets, dates_dev, paths)
    return net_exposure.reshape(shape), funding.reshape(shape)


def solution(mesh):
    return jax.shard_map(
        shards,
        mesh=mesh,
        in_specs=(P("trade", "date", "path"), P("trade"), P(), P(), P()),
        out_specs=(P("trade", "date", "path"), P("trade", "date", "path")),
        check_vma=False,
    )
```

```python
import functools
import math

import jax
import jax.numpy as jnp
from jax import lax
from jax.experimental import pallas as pl
from jax.experimental.pallas import tpu as pltpu
from jax.sharding import PartitionSpec as P


LAG = 10
GRANT = 8 * 1024 * 1024
PARTS = ((2, 2), (2, 2))
ROWS = 32
LEAVING = 8


def ahead(value, axis):
    count = lax.axis_size(axis)
    return lax.ppermute(value, axis, [(i, (i + 1) % count) for i in range(count)])


def exchanged(value, axis, bit):
    return lax.ppermute(value, axis, [(i, i ^ bit) for i in range(lax.axis_size(axis))])


def row_sums(labels, rows, values):
    place = lax.broadcasted_iota(jnp.int32, (rows, labels.shape[0]), 0)
    selector = (place == labels[None, :]).astype(jnp.bfloat16)
    return jnp.einsum("sn,ntp->tsp", selector, values, preferred_element_type=jnp.float32)


def parts_of(sets):
    whole = sum(sum(part) for part in PARTS)
    sizes = [[sets * share // whole for share in part] for part in PARTS]
    assert sum(map(sum, sizes)) == sets
    return sizes


def call(body, operands, shapes, scratch=(), to_hbm=False, into=()):
    vmem, hbm = pl.BlockSpec(memory_space=pltpu.VMEM), pl.BlockSpec(memory_space=pl.ANY)
    moved = sum(a.size for a in operands) + sum(s[0] * s[1] for s in shapes)
    return pl.pallas_call(
        body,
        out_shape=[jax.ShapeDtypeStruct(s, jnp.float32) for s in shapes],
        in_specs=[vmem] * len(operands) + [hbm] * len(into),
        out_specs=[hbm if to_hbm else vmem] * len(shapes),
        scratch_shapes=list(scratch),
        compiler_params=pltpu.CompilerParams(vmem_limit_bytes=GRANT),
        cost_estimate=pl.CostEstimate(flops=8 * moved, bytes_accessed=4 * moved, transcendentals=0),
        input_output_aliases={len(operands) + i: i for i in range(len(into))},
    )(*operands, *into)


def prepare_kernel(rates_ref, level_ref, spread_ref, rate_out, level_out, spread_out, coef_out, slab_ref):
    dates_dev, sets, paths = rate_out.shape
    count, mine = lax.axis_size("date"), lax.axis_index("date")
    trade = lax.axis_index("trade")
    lanes = pl.ds(pl.multiple_of(trade * sets, sets), sets)

    def across(row):
        return jnp.broadcast_to(jnp.transpose(jnp.broadcast_to(row, (8, sets)))[:, :1], (sets, paths))

    here = rates_ref[pl.ds(pl.multiple_of(mine * dates_dev, dates_dev), dates_dev), lanes]
    columns = jnp.transpose(here)
    for t in range(dates_dev):
        rate_out[t] = jnp.broadcast_to(columns[:, t : t + 1], (sets, paths))
    level_out[...] = across(level_ref[pl.ds(trade, 1), :])
    spread_out[...] = across(spread_ref[pl.ds(trade, 1), :])
    for d in range(count):
        total = rates_ref[pl.ds(d * dates_dev, 1), lanes]
        for t in range(1, dates_dev):
            total = total * rates_ref[pl.ds(d * dates_dev + t, 1), lanes]
        slab_ref[pl.ds(d, 1), :] = total

    bit, stage = count // 2, 0
    while bit:
        base = mine - mine % (2 * bit)
        lower = beyond = jnp.ones((1, sets), jnp.float32)
        for i in range(bit):
            rate = slab_ref[pl.ds(base + i, 1), :]
            lower = lower * rate
            beyond = beyond * jnp.where(base + i > mine, rate, 1.0)
        coef_out[2 * stage] = across(lower)
        coef_out[2 * stage + 1] = across(beyond)
        bit, stage = bit // 2, stage + 1


def net(now, lagged, level):
    return now - (jnp.maximum(lagged - level, 0.0) - jnp.maximum(-lagged - level, 0.0))


def each_block(begin, pieces, refs, use):
    own_ref, other_ref = refs[:2]
    late_refs, rim_refs = refs[2 : 2 + pieces], refs[2 + pieces : 2 + 2 * pieces]
    level_ref = refs[2 + 2 * pieces]
    first = lax.axis_index("date") == 0
    early, dates_dev = other_ref.shape[0], own_ref.shape[0]
    at = 0
    for late_ref, rim_ref in zip(late_refs, rim_refs):
        size = math.gcd(ROWS, late_ref.shape[1])
        for row in range(0, late_ref.shape[1], size):
            within, inside, rows = pl.ds(row, size), pl.ds(at, size), pl.ds(begin + at, size)
            level = level_ref[rows, :]
            held, found = [], []
            for t in range(dates_dev):
                if t < early:
                    held.append(own_ref[t, rows, :] + other_ref[t, inside, :])
                else:
                    held.append(late_ref[t - early, within, :])
                lagged = held[t - LAG] if t >= LAG else jnp.where(first, 0.0, rim_ref[t, within, :])
                found.append(net(held[t], lagged, level))
            use(at, size, rows, found)
            at += size


def cost_kernel(begin, pieces, *refs):
    spread_ref, rate_ref, coef_ref, cost_out, last_out, sent_out = refs[3 + 2 * pieces :]

    def use(at, size, rows, found):
        inside = pl.ds(at, size)
        spread = spread_ref[rows, :]
        state = jnp.zeros_like(spread)
        for t, exposure in enumerate(found):
            cost = spread * jnp.maximum(exposure, 0.0)
            cost_out[t, inside, :] = cost
            state = rate_ref[t, rows, :] * state + cost
        last_out[inside, :] = state
        sent_out[inside, :] = state * coef_ref[1, rows, :]

    each_block(begin, pieces, refs, use)


def exposure_kernel(begin, pieces, *refs):
    dates_dev = refs[0].shape[0]

    def use(at, size, rows, found):
        for t, exposure in enumerate(found):
            refs[-1][pl.ds(at * dates_dev + t, size, stride=dates_dev), :] = exposure

    each_block(begin, pieces, refs, use)


def entering(stages, others, coef_ref, inside, rows):
    mine, count = lax.axis_index("date"), lax.axis_size("date")
    arrived = jnp.where(mine >= count // 2, others[0][inside, :], 0.0)
    for stage in range(1, stages):
        upper = mine & (count >> (stage + 1)) != 0
        kept = jnp.where(upper, arrived * coef_ref[2 * stage, rows, :], arrived)
        arrived = kept + others[stage][inside, :]
    return arrived


def join_kernel(begin, stage, last_ref, coef_ref, *refs):
    inside, rows = pl.ds(0, last_ref.shape[0]), pl.ds(begin, last_ref.shape[0])
    arrived = entering(stage, refs[:-1], coef_ref, inside, rows)
    longer = arrived * coef_ref[2 * stage, rows, :] + last_ref[...] * coef_ref[2 * stage + 1, rows, :]
    upper = lax.axis_index("date") & (lax.axis_size("date") >> (stage + 1)) != 0
    refs[-1][...] = jnp.where(upper, arrived, longer)


def funding_kernel(begin, stages, *refs):
    coef_ref, cost_ref, rate_ref, net_ref = refs[stages : stages + 4]
    net_out, out, held_ref, sem = refs[-4:]
    dates_dev, size = cost_ref.shape[:2]
    block = LEAVING * dates_dev

    def leaving(part):
        here, there = pl.ds(part * block, block), pl.ds(begin * dates_dev + part * block, block)
        return pltpu.make_async_copy(held_ref.at[here, :], out.at[there, :], sem.at[part + 1])

    there = pl.ds(begin * dates_dev, size * dates_dev)
    exposed = pltpu.make_async_copy(net_ref, net_out.at[there, :], sem.at[0])
    exposed.start()
    parts = range(size // LEAVING)
    for part in parts:
        inside = pl.ds(part * LEAVING, LEAVING)
        rows = pl.ds(begin + part * LEAVING, LEAVING)
        state = entering(stages, refs[:stages], coef_ref, inside, rows)
        for t in range(dates_dev):
            state = rate_ref[t, rows, :] * state + cost_ref[t, inside, :]
            held_ref[pl.ds(part * block + t, LEAVING, stride=dates_dev), :] = state
        leaving(part).start()
    exposed.wait()
    for part in parts:
        leaving(part).wait()


def shards(trade_values, set_of_trade, thresholds, spreads, retention):
    set_count = thresholds.shape[0]
    dates_dev, paths = trade_values.shape[1:]
    n_trade = lax.axis_size("trade")
    sets = set_count // n_trade
    offset = set_of_trade - lax.axis_index("trade") * sets
    offset = jnp.where(offset < 0, offset + set_count, offset)
    early = dates_dev - LAG
    sizes = parts_of(sets)
    pieces, groups, low = [], [], 0
    for part in sizes:
        groups.append((low, low + sum(part), range(len(pieces), len(pieces) + len(part))))
        for size in part:
            pieces.append(slice(low, low + size))
            low += size

    cross = lax.optimization_barrier(row_sums(offset - sets, sets, trade_values))
    late_in, other = [], []
    for rows in pieces:
        late_in.append(ahead(cross[early:, rows], "trade"))
    for low, high, _ in groups:
        other.append(ahead(cross[:early, low:high], "trade"))
    own = row_sums(offset, sets, trade_values)
    late, rims = [], []
    for k, rows in enumerate(pieces):
        mine = own if k == 0 else lax.optimization_barrier((own, late[-1]))[0]
        sums = mine[early:, rows] + late_in[k]
        rims.append(ahead(sums, "date"))
        late.append(sums)

    count = lax.axis_size("date")
    stages = count.bit_length() - 1
    tall, wide = (dates_dev, sets, paths), (sets, paths)
    rate_all, level_all, spread_all, coefs = call(
        prepare_kernel,
        (retention.T, thresholds.reshape(n_trade, sets), spreads.reshape(n_trade, sets)),
        (tall, wide, wide, (2 * stages, *wide)),
        [pltpu.VMEM((count, sets), jnp.float32)],
    )

    flat = (sets * dates_dev, paths)
    results = ()
    for g, (low, high, mine) in enumerate(groups):
        size = high - low
        parts = (own, other[g], *[late[k] for k in mine], *[rims[k] for k in mine])
        costs, last, sent = call(
            functools.partial(cost_kernel, low, len(mine)),
            (*parts, level_all, spread_all, rate_all, coefs),
            ((dates_dev, size, paths), (size, paths), (size, paths)),
        )
        (exposed,) = call(
            functools.partial(exposure_kernel, low, len(mine)), (*parts, level_all), ((size * dates_dev, paths),)
        )
        others = []
        for stage in range(stages):
            if stage:
                (sent,) = call(functools.partial(join_kernel, low, stage), (last, coefs, *others), ((size, paths),))
            others.append(exchanged(sent, "date", count >> (stage + 1)))
        results = call(
            functools.partial(funding_kernel, low, stages),
            (*others, coefs, costs, rate_all, exposed),
            (flat, flat),
            [pltpu.VMEM((size * dates_dev, paths), jnp.float32), pltpu.SemaphoreType.DMA((1 + size // LEAVING,))],
            True,
            results,
        )
    return tuple(result.reshape(sets, dates_dev, paths) for result in results)


def solution(mesh):
    return jax.shard_map(
        shards,
        mesh=mesh,
        in_specs=(P("trade", "date", "path"), P("trade"), P(), P(), P()),
        out_specs=(P("trade", "date", "path"), P("trade", "date", "path")),
        check_vma=False,
    )
```

```python
import functools
import math

import jax
import jax.numpy as jnp
from jax import lax
from jax.experimental import pallas as pl
from jax.experimental.pallas import tpu as pltpu
from jax.sharding import PartitionSpec as P


LAG = 10
GRANT = 8 * 1024 * 1024
PARTS = ((2, 2), (2, 2))
ROWS = 32
LEAVING = 8


def ahead(value, axis):
    count = lax.axis_size(axis)
    return lax.ppermute(value, axis, [(i, (i + 1) % count) for i in range(count)])


def exchanged(value, axis, bit):
    return lax.ppermute(value, axis, [(i, i ^ bit) for i in range(lax.axis_size(axis))])


def row_sums(labels, rows, values):
    place = lax.broadcasted_iota(jnp.int32, (rows, labels.shape[0]), 0)
    selector = (place == labels[None, :]).astype(jnp.bfloat16)
    return jnp.einsum("sn,ntp->tsp", selector, values, preferred_element_type=jnp.float32)


def parts_of(sets):
    whole = sum(sum(part) for part in PARTS)
    sizes = [[sets * share // whole for share in part] for part in PARTS]
    assert sum(map(sum, sizes)) == sets
    return sizes


def call(body, operands, shapes, scratch=(), to_hbm=False, into=()):
    vmem, hbm = pl.BlockSpec(memory_space=pltpu.VMEM), pl.BlockSpec(memory_space=pl.ANY)
    moved = sum(a.size for a in operands) + sum(s[0] * s[1] for s in shapes)
    return pl.pallas_call(
        body,
        out_shape=[jax.ShapeDtypeStruct(s, jnp.float32) for s in shapes],
        in_specs=[vmem] * len(operands) + [hbm] * len(into),
        out_specs=[hbm if to_hbm else vmem] * len(shapes),
        scratch_shapes=list(scratch),
        compiler_params=pltpu.CompilerParams(vmem_limit_bytes=GRANT),
        cost_estimate=pl.CostEstimate(flops=8 * moved, bytes_accessed=4 * moved, transcendentals=0),
        input_output_aliases={len(operands) + i: i for i in range(len(into))},
    )(*operands, *into)


def prepare_kernel(rates_ref, level_ref, spread_ref, rate_out, level_out, spread_out, coef_out, slab_ref):
    dates_dev, sets, paths = rate_out.shape
    count, mine = lax.axis_size("date"), lax.axis_index("date")
    trade = lax.axis_index("trade")
    lanes = pl.ds(pl.multiple_of(trade * sets, sets), sets)

    def across(row):
        return jnp.broadcast_to(jnp.transpose(jnp.broadcast_to(row, (8, sets)))[:, :1], (sets, paths))

    here = rates_ref[pl.ds(pl.multiple_of(mine * dates_dev, dates_dev), dates_dev), lanes]
    columns = jnp.transpose(here)
    for t in range(dates_dev):
        rate_out[t] = jnp.broadcast_to(columns[:, t : t + 1], (sets, paths))
    level_out[...] = across(level_ref[pl.ds(trade, 1), :])
    spread_out[...] = across(spread_ref[pl.ds(trade, 1), :])
    for d in range(count):
        total = rates_ref[pl.ds(d * dates_dev, 1), lanes]
        for t in range(1, dates_dev):
            total = total * rates_ref[pl.ds(d * dates_dev + t, 1), lanes]
        slab_ref[pl.ds(d, 1), :] = total

    bit, stage = count // 2, 0
    while bit:
        base = mine - mine % (2 * bit)
        lower = beyond = jnp.ones((1, sets), jnp.float32)
        for i in range(bit):
            rate = slab_ref[pl.ds(base + i, 1), :]
            lower = lower * rate
            beyond = beyond * jnp.where(base + i > mine, rate, 1.0)
        coef_out[2 * stage] = across(lower)
        coef_out[2 * stage + 1] = across(beyond)
        bit, stage = bit // 2, stage + 1


def net(now, lagged, level):
    return now - (jnp.maximum(lagged - level, 0.0) - jnp.maximum(-lagged - level, 0.0))


def each_block(begin, pieces, refs, use):
    own_ref, other_ref = refs[:2]
    late_refs, rim_refs = refs[2 : 2 + pieces], refs[2 + pieces : 2 + 2 * pieces]
    level_ref = refs[2 + 2 * pieces]
    first = lax.axis_index("date") == 0
    early, dates_dev = other_ref.shape[0], own_ref.shape[0]
    at = 0
    for late_ref, rim_ref in zip(late_refs, rim_refs):
        size = math.gcd(ROWS, late_ref.shape[1])
        for row in range(0, late_ref.shape[1], size):
            within, inside, rows = pl.ds(row, size), pl.ds(at, size), pl.ds(begin + at, size)
            level = level_ref[rows, :]
            held, found = [], []
            for t in range(dates_dev):
                if t < early:
                    held.append(own_ref[t, rows, :] + other_ref[t, inside, :])
                else:
                    held.append(late_ref[t - early, within, :])
                lagged = held[t - LAG] if t >= LAG else jnp.where(first, 0.0, rim_ref[t, within, :])
                found.append(net(held[t], lagged, level))
            use(at, size, rows, found)
            at += size


def cost_kernel(begin, pieces, *refs):
    spread_ref, rate_ref, coef_ref, cost_out, last_out, sent_out = refs[3 + 2 * pieces :]

    def use(at, size, rows, found):
        inside = pl.ds(at, size)
        spread = spread_ref[rows, :]
        state = jnp.zeros_like(spread)
        for t, exposure in enumerate(found):
            cost = spread * jnp.maximum(exposure, 0.0)
            cost_out[t, inside, :] = cost
            state = rate_ref[t, rows, :] * state + cost
        last_out[inside, :] = state
        sent_out[inside, :] = state * coef_ref[1, rows, :]

    each_block(begin, pieces, refs, use)


def entering(stages, others, coef_ref, inside, rows):
    mine, count = lax.axis_index("date"), lax.axis_size("date")
    arrived = jnp.where(mine >= count // 2, others[0][inside, :], 0.0)
    for stage in range(1, stages):
        upper = mine & (count >> (stage + 1)) != 0
        kept = jnp.where(upper, arrived * coef_ref[2 * stage, rows, :], arrived)
        arrived = kept + others[stage][inside, :]
    return arrived


def join_kernel(begin, stage, last_ref, coef_ref, *refs):
    inside, rows = pl.ds(0, last_ref.shape[0]), pl.ds(begin, last_ref.shape[0])
    arrived = entering(stage, refs[:-1], coef_ref, inside, rows)
    longer = arrived * coef_ref[2 * stage, rows, :] + last_ref[...] * coef_ref[2 * stage + 1, rows, :]
    upper = lax.axis_index("date") & (lax.axis_size("date") >> (stage + 1)) != 0
    refs[-1][...] = jnp.where(upper, arrived, longer)


def accumulate(begin, size, others, coef_ref, cost_ref, rate_ref, out, held_ref, sem):
    dates_dev = rate_ref.shape[0]
    block = LEAVING * dates_dev
    copies = []
    for part in range(size // LEAVING):
        low = begin + part * LEAVING
        inside, rows = pl.ds(part * LEAVING, LEAVING), pl.ds(low, LEAVING)
        if others:
            state = entering(len(others), others, coef_ref, inside, rows)
        else:
            state = jnp.zeros_like(coef_ref[0, rows, :])
        for t in range(dates_dev):
            state = rate_ref[t, rows, :] * state + cost_ref[t, inside, :]
            held_ref[pl.ds(low * dates_dev + t, LEAVING, stride=dates_dev), :] = state
        here = pl.ds(low * dates_dev, block)
        copies.append(pltpu.make_async_copy(held_ref.at[here, :], out.at[here, :], sem.at[low // LEAVING]))
        copies[-1].start()
    return copies


def settle_kernel(groups, stages, *refs):
    refs = list(refs)
    net_out, out, net_ref, held_ref, net_sem, sem = refs[-6:]
    own_ref, level_ref, coef_ref, rate_ref = refs[:4]
    cost_refs = refs[4 : 4 + len(groups)]
    at = 4 + len(groups)
    dates_dev = rate_ref.shape[0]
    arrived = []
    for _ in groups[:-1]:
        arrived.append(refs[at : at + stages])
        at += stages
    copies = []
    for low, high, mine in groups:
        count = 1 + 2 * len(mine)
        parts = [own_ref, *refs[at : at + count], level_ref]
        at += count

        def use(row, size, rows, found, low=low):
            for t, exposure in enumerate(found):
                net_ref[pl.ds((low + row) * dates_dev + t, size, stride=dates_dev), :] = exposure
            here = pl.ds((low + row) * dates_dev, size * dates_dev)
            copies.append(pltpu.make_async_copy(net_ref.at[here, :], net_out.at[here, :], net_sem.at[len(copies)]))
            copies[-1].start()

        each_block(low, len(mine), parts, use)
    for (low, high, _), cost_ref, others in zip(groups, cost_refs, arrived):
        copies += accumulate(low, high - low, others, coef_ref, cost_ref, rate_ref, out, held_ref, sem)

    @pl.when(lax.axis_index("date") == 0)
    def _():
        low, high, _ = groups[-1]
        for copy in accumulate(low, high - low, (), coef_ref, cost_refs[-1], rate_ref, out, held_ref, sem):
            copy.wait()

    for copy in copies:
        copy.wait()


def funding_kernel(low, high, stages, *refs):
    coef_ref, cost_ref, rate_ref = refs[stages : stages + 3]
    out, held_ref, sem = refs[-3:]

    @pl.when(lax.axis_index("date") != 0)
    def _():
        for copy in accumulate(low, high - low, refs[:stages], coef_ref, cost_ref, rate_ref, out, held_ref, sem):
            copy.wait()


def shards(trade_values, set_of_trade, thresholds, spreads, retention):
    set_count = thresholds.shape[0]
    dates_dev, paths = trade_values.shape[1:]
    n_trade = lax.axis_size("trade")
    sets = set_count // n_trade
    offset = set_of_trade - lax.axis_index("trade") * sets
    offset = jnp.where(offset < 0, offset + set_count, offset)
    early = dates_dev - LAG
    sizes = parts_of(sets)
    pieces, groups, low = [], [], 0
    for part in sizes:
        groups.append((low, low + sum(part), range(len(pieces), len(pieces) + len(part))))
        for size in part:
            pieces.append(slice(low, low + size))
            low += size

    cross = lax.optimization_barrier(row_sums(offset - sets, sets, trade_values))
    late_in, other = [], []
    for rows in pieces:
        late_in.append(ahead(cross[early:, rows], "trade"))
    for low, high, _ in groups:
        other.append(ahead(cross[:early, low:high], "trade"))
    own = row_sums(offset, sets, trade_values)
    late, rims = [], []
    for k, rows in enumerate(pieces):
        mine = own if k == 0 else lax.optimization_barrier((own, late[-1]))[0]
        sums = mine[early:, rows] + late_in[k]
        rims.append(ahead(sums, "date"))
        late.append(sums)

    count = lax.axis_size("date")
    stages = count.bit_length() - 1
    tall, wide = (dates_dev, sets, paths), (sets, paths)
    rate_all, level_all, spread_all, coefs = call(
        prepare_kernel,
        (retention.T, thresholds.reshape(n_trade, sets), spreads.reshape(n_trade, sets)),
        (tall, wide, wide, (2 * stages, *wide)),
        [pltpu.VMEM((count, sets), jnp.float32)],
    )

    flat = (sets * dates_dev, paths)
    costs, arrived, inputs = [], [], []
    for g, (low, high, mine) in enumerate(groups):
        size = high - low
        parts = (other[g], *[late[k] for k in mine], *[rims[k] for k in mine])
        inputs += parts
        cost, last, sent = call(
            functools.partial(cost_kernel, low, len(mine)),
            (own, *parts, level_all, spread_all, rate_all, coefs),
            ((dates_dev, size, paths), (size, paths), (size, paths)),
        )
        costs.append(cost)
        others = []
        for stage in range(stages):
            if stage:
                (sent,) = call(functools.partial(join_kernel, low, stage), (last, coefs, *others), ((size, paths),))
            others.append(exchanged(sent, "date", count >> (stage + 1)))
        arrived.append(others)

    held, leaving = pltpu.VMEM(flat, jnp.float32), pltpu.SemaphoreType.DMA((sets // LEAVING,))
    early_carries = [part for others in arrived[:-1] for part in others]
    net_exposure, funding = call(
        functools.partial(settle_kernel, groups, stages),
        (own, level_all, coefs, rate_all, *costs, *early_carries, *inputs),
        (flat, flat),
        [held, held, leaving, leaving],
        True,
    )
    low, high, _ = groups[-1]
    (funding,) = call(
        functools.partial(funding_kernel, low, high, stages),
        (*arrived[-1], coefs, costs[-1], rate_all),
        (flat,),
        [held, leaving],
        True,
        (funding,),
    )
    return tuple(result.reshape(sets, dates_dev, paths) for result in (net_exposure, funding))


def solution(mesh):
    return jax.shard_map(
        shards,
        mesh=mesh,
        in_specs=(P("trade", "date", "path"), P("trade"), P(), P(), P()),
        out_specs=(P("trade", "date", "path"), P("trade", "date", "path")),
        check_vma=False,
    )
```

```python
import functools
import itertools
import math

import jax
import jax.numpy as jnp
from jax import lax
from jax.experimental import pallas as pl
from jax.experimental.pallas import tpu as pltpu
from jax.sharding import PartitionSpec as P


LAG = 10
GRANT = 8 * 1024 * 1024
PARTS = ((2, 2, 2, 2),)
ROWS = 32
LEAVING = 8
RINGS = 4


def ahead(value, axis):
    count = lax.axis_size(axis)
    return lax.ppermute(value, axis, [(i, (i + 1) % count) for i in range(count)])


def exchanged(value, axis, bit):
    return lax.ppermute(value, axis, [(i, i ^ bit) for i in range(lax.axis_size(axis))])


def halved(value, axis, move, upper):
    names = ("trade", "date", "path")
    counts = [lax.axis_size(name) for name in names]
    which, half = names.index(axis), counts[1] // 2
    pairs = []
    for place in itertools.product(*map(range, counts)):
        goal = list(place)
        moved = move(place[which], counts[which])
        if upper in (None, place[1] >= half) and 0 <= moved < counts[which]:
            goal[which] = moved
        elif place[2] ^ 1 < counts[2]:
            goal[2] = place[2] ^ 1
        pairs.append((index_of(place, counts), index_of(goal, counts)))
    return lax.ppermute(value, names, pairs)


def index_of(place, counts):
    return (place[0] * counts[1] + place[1]) * counts[2] + place[2]


def row_sums(labels, rows, values):
    place = lax.broadcasted_iota(jnp.int32, (rows, labels.shape[0]), 0)
    selector = (place == labels[None, :]).astype(jnp.bfloat16)
    return jnp.einsum("sn,ntp->tsp", selector, values, preferred_element_type=jnp.float32)


def parts_of(sets):
    whole = sum(sum(part) for part in PARTS)
    sizes = [[sets * share // whole for share in part] for part in PARTS]
    assert sum(map(sum, sizes)) == sets
    return sizes


def call(body, operands, shapes, scratch=(), to_hbm=False, into=()):
    vmem, hbm = pl.BlockSpec(memory_space=pltpu.VMEM), pl.BlockSpec(memory_space=pl.ANY)
    moved = sum(a.size for a in operands) + sum(s[0] * s[1] for s in shapes)
    return pl.pallas_call(
        body,
        out_shape=[jax.ShapeDtypeStruct(s, jnp.float32) for s in shapes],
        in_specs=[vmem] * len(operands) + [hbm] * len(into),
        out_specs=[hbm if to_hbm else vmem] * len(shapes),
        scratch_shapes=list(scratch),
        compiler_params=pltpu.CompilerParams(vmem_limit_bytes=GRANT),
        cost_estimate=pl.CostEstimate(flops=8 * moved, bytes_accessed=4 * moved, transcendentals=0),
        input_output_aliases={len(operands) + i: i for i in range(len(into))},
    )(*operands, *into)


def prepare_kernel(rates_ref, level_ref, spread_ref, rate_out, level_out, spread_out, coef_out, slab_ref):
    dates_dev, sets, paths = rate_out.shape
    count, mine = lax.axis_size("date"), lax.axis_index("date")
    trade = lax.axis_index("trade")
    lanes = pl.ds(pl.multiple_of(trade * sets, sets), sets)

    def across(row):
        return jnp.broadcast_to(jnp.transpose(jnp.broadcast_to(row, (8, sets)))[:, :1], (sets, paths))

    here = rates_ref[pl.ds(pl.multiple_of(mine * dates_dev, dates_dev), dates_dev), lanes]
    columns = jnp.transpose(here)
    for t in range(dates_dev):
        rate_out[t] = jnp.broadcast_to(columns[:, t : t + 1], (sets, paths))
    level_out[...] = across(level_ref[pl.ds(trade, 1), :])
    spread_out[...] = across(spread_ref[pl.ds(trade, 1), :])
    for d in range(count):
        total = rates_ref[pl.ds(d * dates_dev, 1), lanes]
        for t in range(1, dates_dev):
            total = total * rates_ref[pl.ds(d * dates_dev + t, 1), lanes]
        slab_ref[pl.ds(d, 1), :] = total

    bit, stage = count // 2, 0
    while bit:
        base = mine - mine % (2 * bit)
        lower = beyond = jnp.ones((1, sets), jnp.float32)
        for i in range(bit):
            rate = slab_ref[pl.ds(base + i, 1), :]
            lower = lower * rate
            beyond = beyond * jnp.where(base + i > mine, rate, 1.0)
        coef_out[2 * stage] = across(lower)
        coef_out[2 * stage + 1] = across(beyond)
        bit, stage = bit // 2, stage + 1


def net(now, lagged, level):
    return now - (jnp.maximum(lagged - level, 0.0) - jnp.maximum(-lagged - level, 0.0))


def upper_half():
    return lax.axis_index("date") >= lax.axis_size("date") // 2


def each_block(begin, own_ref, other_ref, late_refs, rim_refs, level_ref, use):
    mine = lax.axis_index("date")
    first, odd = mine == 0, mine % 2 == 1
    early, dates_dev = other_ref.shape[0], own_ref.shape[0]
    at = 0
    for late_ref, rims in zip(late_refs, rim_refs):
        size = math.gcd(ROWS, late_ref.shape[1])
        for row in range(0, late_ref.shape[1], size):
            within, inside, rows = pl.ds(row, size), pl.ds(at, size), pl.ds(begin + at, size)
            level = level_ref[rows, :]
            held, found = [], []
            for t in range(dates_dev):
                if t < early:
                    held.append(own_ref[t, rows, :] + other_ref[t, inside, :])
                else:
                    held.append(late_ref[t - early, within, :])
                if t >= LAG:
                    lagged = held[t - LAG]
                else:
                    lagged = rims[0][t, within, :]
                    if len(rims) > 1:
                        lagged = jnp.where(odd, lagged, rims[1][t, within, :])
                    lagged = jnp.where(first, 0.0, lagged)
                found.append(net(held[t], lagged, level))
            use(at, size, rows, found)
            at += size


def on_half(half):
    return upper_half() if half == "upper" else jnp.logical_not(upper_half())


def taker(refs):
    rest = list(refs)

    def take(number):
        taken = rest[:number]
        del rest[:number]
        return taken

    return take


def cost_kernel(begin, kinds, half, *refs):
    take = taker(refs)
    own_ref, other_ref, level_ref, spread_ref, rate_ref, coef_ref = take(6)
    late_refs, rim_refs = take(len(kinds)), [take(kind) for kind in kinds]
    cost_out, *ends = take(3)

    def use(at, size, rows, found):
        inside = pl.ds(at, size)
        spread = spread_ref[rows, :]
        state = jnp.zeros_like(spread)
        for t, exposure in enumerate(found):
            cost = spread * jnp.maximum(exposure, 0.0)
            cost_out[t, inside, :] = cost
            state = rate_ref[t, rows, :] * state + cost
        ends[0][inside, :] = state
        if half == "lower":
            ends[1][inside, :] = state * coef_ref[1, rows, :]

    @pl.when(on_half(half))
    def _():
        each_block(begin, own_ref, other_ref, late_refs, rim_refs, level_ref, use)

    @pl.when(jnp.logical_not(on_half(half)))
    def _():
        for end in ends:
            end[...] = jnp.zeros_like(end)


def entering(half, others, coef_ref, inside, rows):
    mine, count = lax.axis_index("date"), lax.axis_size("date")
    stage = 1
    if half == "lower":
        arrived, later = jnp.zeros_like(coef_ref[0, rows, :]), others
    else:
        arrived, later = others[0][inside, :], others[1:]
    for other in later:
        upper = mine & (count >> (stage + 1)) != 0
        kept = jnp.where(upper, arrived * coef_ref[2 * stage, rows, :], arrived)
        arrived = kept + other[inside, :]
        stage += 1
    return arrived


def join_kernel(begin, stage, half, last_ref, coef_ref, *refs):
    inside, rows = pl.ds(0, last_ref.shape[0]), pl.ds(begin, last_ref.shape[0])
    arrived = entering(half, refs[:-1], coef_ref, inside, rows)
    longer = arrived * coef_ref[2 * stage, rows, :] + last_ref[...] * coef_ref[2 * stage + 1, rows, :]
    upper = lax.axis_index("date") & (lax.axis_size("date") >> (stage + 1)) != 0
    refs[-1][...] = jnp.where(upper, arrived, longer)


def accumulate(begin, size, half, others, coef_ref, cost_ref, rate_ref, out, held_ref, sem):
    dates_dev = rate_ref.shape[0]
    block = LEAVING * dates_dev
    copies = []
    for part in range(size // LEAVING):
        low = begin + part * LEAVING
        inside, rows = pl.ds(part * LEAVING, LEAVING), pl.ds(low, LEAVING)
        state = entering(half, others, coef_ref, inside, rows)
        for t in range(dates_dev):
            state = rate_ref[t, rows, :] * state + cost_ref[t, inside, :]
            held_ref[pl.ds(low * dates_dev + t, LEAVING, stride=dates_dev), :] = state
        here = pl.ds(low * dates_dev, block)
        copies.append(pltpu.make_async_copy(held_ref.at[here, :], out.at[here, :], sem.at[low // LEAVING]))
        copies[-1].start()
    return copies


def settle_kernel(groups, kinds, counts, *refs):
    net_out, out, net_ref, held_ref, net_sem, sem = refs[-6:]
    take = taker(refs[:-6])
    own_ref, level_ref, coef_ref, rate_ref = take(4)
    late_refs, rim_refs = take(len(kinds)), [take(kind) for kind in kinds]
    dates_dev = rate_ref.shape[0]

    def finish(half, ready, parts):
        copies = []
        for (low, _, mine), (other_ref, _, _) in zip(groups, parts):

            def use(row, size, rows, found, low=low):
                for t, exposure in enumerate(found):
                    net_ref[pl.ds((low + row) * dates_dev + t, size, stride=dates_dev), :] = exposure
                here = pl.ds((low + row) * dates_dev, size * dates_dev)
                copies.append(pltpu.make_async_copy(net_ref.at[here, :], net_out.at[here, :], net_sem.at[len(copies)]))
                copies[-1].start()

            lates, rims = [late_refs[k] for k in mine], [rim_refs[k] for k in mine]
            each_block(low, own_ref, other_ref, lates, rims, level_ref, use)
        for (low, high, _), (_, cost_ref, others) in zip(groups[:ready], parts):
            copies.extend(
                accumulate(low, high - low, half, others, coef_ref, cost_ref, rate_ref, out, held_ref, sem)
            )
        for copy in copies:
            copy.wait()

    for half, numbers in counts:
        parts = [(take(1)[0], take(1)[0], take(number)) for number in numbers]
        first = lax.axis_index("date") == 0
        if half == "upper":
            turn, ready = upper_half(), len(groups) - 1
        else:
            turn, ready = jnp.logical_and(on_half("lower"), jnp.logical_not(first)), len(groups)
            if len(counts) == 1:
                turn = first
        pl.when(turn)(functools.partial(finish, half, ready, parts))


def funding_kernel(low, high, *refs):
    coef_ref, rate_ref, cost_ref = refs[:3]
    out, held_ref, sem = refs[-3:]

    @pl.when(upper_half())
    def _():
        for copy in accumulate(low, high - low, "upper", refs[3:-4], coef_ref, cost_ref, rate_ref, out, held_ref, sem):
            copy.wait()


def shards(trade_values, set_of_trade, thresholds, spreads, retention):
    set_count = thresholds.shape[0]
    dates_dev, paths = trade_values.shape[1:]
    n_trade = lax.axis_size("trade")
    sets = set_count // n_trade
    offset = set_of_trade - lax.axis_index("trade") * sets
    offset = jnp.where(offset < 0, offset + set_count, offset)
    early = dates_dev - LAG
    sizes = parts_of(sets)
    pieces, groups, low = [], [], 0
    for part in sizes:
        groups.append((low, low + sum(part), range(len(pieces), len(pieces) + len(part))))
        for size in part:
            pieces.append(slice(low, low + size))
            low += size

    cross = lax.optimization_barrier(row_sums(offset - sets, sets, trade_values))
    late_in, other = [], []
    for rows in pieces:
        late_in.append(ahead(cross[early:, rows], "trade"))
    halves = ("lower", "upper")
    for low, high, _ in groups:
        ends = {}
        for half in halves:
            part = cross[:early, low:high]
            ends[half] = halved(part, "trade", lambda i, n: (i + 1) % n, half == "upper")
        other.append(ends)
    own = row_sums(offset, sets, trade_values)
    late, rims = [], []
    for k, rows in enumerate(pieces):
        mine = own if k == 0 else lax.optimization_barrier((own, late[-1]))[0]
        sums = mine[early:, rows] + late_in[k]
        if k < RINGS:
            rims.append((ahead(sums, "date"),))
        else:
            behind = [lambda i, n: i ^ 1, lambda i, n: ((i + 1) ^ 1) - 1]
            rims.append(tuple(halved(sums, "date", move, None) for move in behind))
        late.append(sums)

    count = lax.axis_size("date")
    stages = count.bit_length() - 1
    tall, wide = (dates_dev, sets, paths), (sets, paths)
    rate_all, level_all, spread_all, coefs = call(
        prepare_kernel,
        (retention.T, thresholds.reshape(n_trade, sets), spreads.reshape(n_trade, sets)),
        (tall, wide, wide, (2 * stages, *wide)),
        [pltpu.VMEM((count, sets), jnp.float32)],
    )

    flat = (sets * dates_dev, paths)
    kinds = [len(rim) for rim in rims]
    costs, carries = [], []
    for g, (low, high, mine) in enumerate(groups):
        size = high - low
        parts = (*[late[k] for k in mine], *[rim for k in mine for rim in rims[k]])
        found, arrived = {}, {}
        for half in halves:
            found[half], last, *sending = call(
                functools.partial(cost_kernel, low, [kinds[k] for k in mine], half),
                (own, other[g][half], level_all, spread_all, rate_all, coefs, *parts),
                ((dates_dev, size, paths), *[(size, paths)] * (2 if half == "lower" else 1)),
            )
            if half == "lower":
                far = exchanged(sending[0], "date", count >> 1)
            others = [] if half == "lower" else [far]
            for stage in range(1, stages):
                body = functools.partial(join_kernel, low, stage, half)
                (sent,) = call(body, (last, coefs, *others), ((size, paths),))
                bit = count >> (stage + 1)
                others.append(halved(sent, "date", lambda i, n, bit=bit: i ^ bit, half == "upper"))
            arrived[half] = others
        costs.append(found)
        carries.append(arrived)

    held, leaving = pltpu.VMEM(flat, jnp.float32), pltpu.SemaphoreType.DMA((sets // LEAVING,))
    shared = (own, level_all, coefs, rate_all, *late, *[part for rim in rims for part in rim])

    def settled(chosen, results):
        counts, inputs = [], []
        for half in chosen:
            numbers = []
            for g in range(len(groups)):
                waits = [] if len(chosen) == 1 or (half == "upper" and g + 1 == len(groups)) else carries[g][half]
                numbers.append(len(waits))
                inputs += [other[g][half], costs[g][half], *waits]
            counts.append((half, numbers))
        return call(
            functools.partial(settle_kernel, groups, kinds, counts),
            (*shared, *inputs),
            (flat, flat),
            [held, held, leaving, leaving],
            True,
            results,
        )

    results = settled(halves, settled(halves[:1], ()))
    net_exposure, funding = results
    low, high, _ = groups[-1]
    (funding,) = call(
        functools.partial(funding_kernel, low, high),
        (coefs, rate_all, costs[-1]["upper"], *carries[-1]["upper"]),
        (flat,),
        [held, leaving],
        True,
        (funding,),
    )
    return tuple(result.reshape(sets, dates_dev, paths) for result in (net_exposure, funding))


def solution(mesh):
    return jax.shard_map(
        shards,
        mesh=mesh,
        in_specs=(P("trade", "date", "path"), P("trade"), P(), P(), P()),
        out_specs=(P("trade", "date", "path"), P("trade", "date", "path")),
        check_vma=False,
    )
```
